512 devices in a mesh: sub: 128 (over z, x, core), blk: 4 (over y).
Axes of the slice: x: 4, y: 4, z: 16, core: 2. Of those that a mesh axis runs over, the one named last changes fastest.
Arguments:
- factor: bfloat16 [256, 2048, 2048], P('sub', None, 'blk'), may hold values from -0.125 to 0.125
- samples: bfloat16 [256, 2048, 128], P('sub', 'blk'), may hold values from -6 to 6
- diagonal: bfloat16 [256, 128, 16], P('sub'), may hold values from 0.25 to 1
- coupling: bfloat16 [256, 64, 2048], P('sub', 'blk'), may hold values from -0.125 to 0.125
- blocks: int32 [256], P('sub'), may hold values from 80 to 128, as said below
- peer_device: int32 [256, 128], P('sub'), may hold values from 0 to 127, as said below
- peer_lane: int32 [256, 128], P('sub'), may hold values from 0 to 1, as said below
- owns_face: int32 [256, 128], P('sub'), may hold values from 0 to 1, as said below
Outputs:
- interior: bfloat16 [256, 64, 128], P('sub', 'blk')
The draws below stay inside these ranges and needn't reach their ends.
Inputs may be any that keep to these rules, and one draw needn't show every extreme that they name: Each subdomain's interface has blocks face blocks; over the subdomains of one index of sub they sum to 208. `peer_device`: live slots are matched in pairs of partners as the statement says, one owning side each; each index of sub owns 104 faces and holds 104 faces owned elsewhere; all faces between two indices of sub are owned by the same one of them; slots that are not live hold 0. Live slots of one index of sub with the same peer_device and the same owns_face have different peer_lane; slots that are not live hold 0. `owns_face`: slots that are not live hold 0.
All inputs are finite; a program needn't handle non-finite values.
Results may differ from the reference program's by a relative error of at most 0.013.
Values may be sent and summed in bfloat16 or wider, within the bound.
No kernel may reach another device: no remote copies, remote signals or barrier semaphores. Data moves between devices by JAX's collectives and lax.ppermute only.
A program may use at most 64 MiB of HBM per device.

```python
import math
import jax
import jax.numpy as jnp
from jax import lax

TILE = 16
MAXB = 128
SUB_DEV = 2
NI = 64
MIDB = 104
ORDER = 2048
COLS = 128
SUBS = 256
FACE_HALF = 104
HALF_CYCLE = 63
CAP = 2
N_SUB = 128
N_BLK = 4


def face_plan(key):
    folded = jax.random.fold_in(key, 29)
    subkeys = jax.random.split(folded, 5)
    placing = jax.random.permutation(subkeys[0], N_SUB).astype(jnp.int32)
    position = jnp.zeros((N_SUB,), jnp.int32).at[placing].set(jnp.arange(N_SUB, dtype=jnp.int32))
    spread_most = MAXB - MIDB
    pair_count = SUB_DEV // 2
    spreads = jax.random.randint(subkeys[1], (N_SUB, pair_count), 0, spread_most + 1).astype(jnp.int32)
    forced = jax.random.randint(subkeys[2], (), 0, N_SUB)
    spreads = spreads.at[forced, 0].set(spread_most)
    shifts = jnp.zeros((N_SUB, SUB_DEV), jnp.int32)
    shifts = shifts.at[:, 0:2 * pair_count:2].set(spreads)
    shifts = shifts.at[:, 1:2 * pair_count:2].set(-spreads)
    orders = jax.vmap(lambda subkey: jax.random.permutation(subkey, SUB_DEV))(jax.random.split(subkeys[3], N_SUB)).astype(jnp.int32)
    shifts = jnp.take_along_axis(shifts, orders, axis=1)
    counts = MIDB + shifts
    end_order = jax.vmap(lambda subkey: jax.random.permutation(subkey, 2 * FACE_HALF))(jax.random.split(subkeys[4], N_SUB)).astype(jnp.int32)
    starts = jnp.cumsum(counts, axis=1) - counts
    slot_index = jnp.arange(MAXB, dtype=jnp.int32)
    ordinal = starts[:, :, None] + slot_index[None, None, :]
    live_slot = slot_index[None, None, :] < counts[:, :, None]
    ordinal = jnp.minimum(ordinal, 2 * FACE_HALF - 1)
    face_end = jnp.take_along_axis(end_order, ordinal.reshape(N_SUB, SUB_DEV * MAXB), axis=1).reshape(N_SUB, SUB_DEV, MAXB)
    owned_end = face_end < FACE_HALF
    face_number = jnp.where(owned_end, face_end, face_end - FACE_HALF)
    cycle_offset = 1 + face_number % HALF_CYCLE
    lane_index = face_number // HALF_CYCLE
    cycle_step = jnp.where(owned_end, cycle_offset, -cycle_offset)
    target = (position[:, None, None] + cycle_step) % N_SUB
    peer_found = placing[target]
    peer_found = jnp.where(live_slot, peer_found, jnp.zeros_like(peer_found)).reshape(SUBS, MAXB).astype(jnp.int32)
    lane_index = jnp.where(live_slot, lane_index, jnp.zeros_like(lane_index)).reshape(SUBS, MAXB).astype(jnp.int32)
    owner_flag = jnp.where(live_slot & owned_end, 1, 0).reshape(SUBS, MAXB).astype(jnp.int32)
    return (counts.reshape(SUBS).astype(jnp.int32), peer_found, lane_index, owner_flag)


def draw_blocks(key, part):
    return face_plan(key)[0]


def draw_peer_device(key, part):
    return face_plan(key)[1]


def draw_peer_lane(key, part):
    return face_plan(key)[2]


def draw_owns_face(key, part):
    return face_plan(key)[3]


def shard_levels(key, dims, shards, least, high):
    factor_of, own = 1.0, jax.random.fold_in(key, 6)
    for dim, shards_of in shards:
        draws = jnp.exp(jax.random.uniform(jax.random.fold_in(own, dim), (shards_of,), jnp.float32, least / len(shards), high / len(shards)))
        factor_of = factor_of * jnp.repeat(draws, dims[dim] // shards_of).reshape([-1 if axis == dim else 1 for axis in range(len(dims))])
    return factor_of


def centred(key, dims, width, limit, shards=(), kind=jnp.bfloat16):
    factor_of = shard_levels(key, dims, shards, -0.22, 0.18) if shards else 1.0
    values = jax.random.normal(key, dims, jnp.float32) * width * factor_of
    return jnp.minimum(jnp.maximum(values, -limit), limit).astype(kind)


def setup_inputs(seed: int = 0) -> dict:
    seeds = jax.random.split(jax.random.key(seed), 9)
    factor = centred(seeds[0], (SUBS, ORDER, ORDER), ORDER ** -0.5, 0.125, ((0, 128), (2, 4)))
    samples = centred(seeds[1], (SUBS, ORDER, COLS), 1.0, 6.0, ((0, 128), (1, 4)))
    diagonal = jnp.clip(jnp.exp(math.log(1.0) - 1.3862944 * jax.random.uniform(seeds[2], (SUBS, MAXB, TILE), jnp.float32) ** shard_levels(seeds[2], (SUBS, MAXB, TILE), ((0, 128),), -0.2, 0.2)), 0.25, 1.0).astype(jnp.bfloat16)
    coupling = centred(seeds[3], (SUBS, NI, ORDER), ORDER ** -0.5, 0.125, ((0, 128), (1, 4)))
    blocks = draw_blocks(jax.random.fold_in(seeds[8], 71), 0)
    peer_device = draw_peer_device(jax.random.fold_in(seeds[8], 71), 0)
    peer_lane = draw_peer_lane(jax.random.fold_in(seeds[8], 71), 0)
    owns_face = draw_owns_face(jax.random.fold_in(seeds[8], 71), 0)
    return dict(factor=factor, samples=samples, diagonal=diagonal, coupling=coupling, blocks=blocks, peer_device=peer_device, peer_lane=peer_lane, owns_face=owns_face)


def apply_factor(operands):
    factor_one, sample_one, count_one = operands
    row_index = jnp.arange(ORDER, dtype=jnp.int32)
    live_rows = row_index < count_one * TILE
    driven = jnp.where(live_rows[:, None], sample_one, jnp.zeros_like(sample_one))
    factor_wide = factor_one.astype(jnp.float32)
    reduced = jnp.dot(factor_wide.T, driven.astype(jnp.float32), preferred_element_type=jnp.float32, precision=lax.Precision.HIGHEST).astype(jnp.bfloat16)
    reduced = jnp.where(live_rows[:, None], reduced, jnp.zeros_like(reduced))
    quarter = ORDER // N_BLK
    running = jnp.zeros((ORDER, COLS), jnp.float32)
    for piece_index in range(N_BLK):
        lower = piece_index * quarter
        product = jnp.dot(factor_wide[:, lower:lower + quarter], reduced[lower:lower + quarter].astype(jnp.float32), preferred_element_type=jnp.float32, precision=lax.Precision.HIGHEST)
        rounded = lax.optimization_barrier(product.astype(jnp.bfloat16))
        running = running + rounded.astype(jnp.float32)
    return running.astype(jnp.bfloat16)


def recover(operands):
    coupling_one, coef_one = operands
    product = jnp.dot(coupling_one.astype(jnp.float32), coef_one.astype(jnp.float32), preferred_element_type=jnp.float32, precision=lax.Precision.HIGHEST)
    return product.astype(jnp.bfloat16)


def reference(factor, samples, diagonal, coupling, blocks, peer_device, peer_lane, owns_face):
    traces = lax.map(apply_factor, (factor, samples, blocks))
    slot_total = SUBS * MAXB
    slot_traces = traces.reshape(slot_total, TILE, COLS).astype(jnp.float32)
    slot_diag = diagonal.reshape(slot_total, TILE).astype(jnp.float32)
    slot_index = jnp.arange(slot_total, dtype=jnp.int32)
    device_of = (slot_index // MAXB) // SUB_DEV
    position = slot_index % MAXB
    live_slot = position < jnp.repeat(blocks, MAXB)
    peers = peer_device.reshape(-1)
    lanes = peer_lane.reshape(-1)
    owning = owns_face.reshape(-1)
    table_size = N_SUB * N_SUB * CAP * 2
    own_key = ((device_of * N_SUB + peers) * CAP + lanes) * 2 + owning
    own_key = jnp.where(live_slot, own_key, table_size)
    table = jnp.zeros((table_size + 1,), jnp.int32).at[own_key].set(slot_index)
    wanted = ((peers * N_SUB + device_of) * CAP + lanes) * 2 + (1 - owning)
    wanted = jnp.where(live_slot, wanted, table_size)
    partner = table[wanted]
    summed = slot_traces + slot_traces[partner]
    divisor = slot_diag + slot_diag[partner]
    coef = (summed / divisor[:, :, None]).astype(jnp.bfloat16)
    coef = jnp.where(live_slot[:, None, None], coef, jnp.zeros_like(coef))
    coefficients = coef.reshape(SUBS, ORDER, COLS)
    return lax.map(recover, (coupling, coefficients))
```

```python
import jax
import jax.numpy as jnp
from jax import lax
from jax.experimental import pallas as pl
from jax.experimental.pallas import tpu as pltpu
from jax.sharding import PartitionSpec as P


BF16 = jnp.bfloat16
F32 = jnp.float32
LANES = 2
BLK = 4
TILE = 16
PART = TILE // BLK
MEMBERS = LANES * PART
PAY = MEMBERS + 2

VMEM = pltpu.VMEM
TN = (((0,), (0,)), ((), ()))
NT = (((1,), (1,)), ((), ()))


def one_hot(target_ref, positions):
    slots = target_ref.shape[1]
    rows = lax.broadcasted_iota(jnp.int32, (positions, slots), 0)
    hit = rows == jnp.broadcast_to(target_ref[...], (positions, slots))
    return jnp.where(hit, 1.0, 0.0).astype(BF16)


def traces_kernel(meta, target, d0, d1, d2, d3, factor, o0, o1, o2, o3, fac, wide, placed, sems):
    subs, order, quarter = factor.shape
    slots = target.shape[1]
    positions = placed.shape[1] // PART
    peers = positions // LANES
    here = meta[0]
    offsets = [pl.multiple_of(lax.rem(here + j, BLK) * quarter, quarter) for j in range(BLK)]
    copies = []
    for s in range(subs):
        for j in range(BLK):
            rows = pl.ds(offsets[j], quarter)
            copy = pltpu.make_async_copy(
                factor.at[s, rows, :], fac.at[s, rows, :], sems.at[s * BLK + j]
            )
            copy.start()
            copies.append(copy)
    for s in range(subs):
        live = meta[1 + s]
        acc = jnp.zeros((d0.shape[2], quarter), F32)
        for j, shard in enumerate((d0, d1, d2, d3)):
            rows = offsets[j] + lax.broadcasted_iota(jnp.int32, shard.shape[1:], 0)
            part = jnp.where(rows < live, shard[s].astype(F32), 0.0).astype(BF16)
            copies[s * BLK + j].wait()
            acc += lax.dot_general(
                part, fac[s, pl.ds(offsets[j], quarter), :], TN, preferred_element_type=F32
            )
        cols = offsets[0] + lax.broadcasted_iota(jnp.int32, acc.shape, 1)
        reduced = jnp.where(cols < live, acc, 0.0).astype(BF16)
        wide[pl.ds(s * order, order), :] = lax.dot_general(
            fac[s], reduced, NT, preferred_element_type=F32
        )
    pick = one_hot(target, positions)
    for t in range(TILE):
        rows = wide[pl.ds(t, slots, stride=TILE), :].astype(BF16)
        moved = jnp.dot(pick, rows, preferred_element_type=F32)
        for lane in range(LANES):
            placed[t // PART, pl.ds(lane * PART + t % PART, peers, stride=MEMBERS), :] = moved[
                lane * peers : (lane + 1) * peers
            ]
    for j, out in enumerate((o0, o1, o2, o3)):
        out[...] = placed[lax.rem(here + j, BLK)].astype(BF16)


def coupling_kernel(meta, target, diag, c0, c1, c2, c3, moved_ref, diag_ref):
    here = meta[0]
    slots = target.shape[1]
    peers = diag_ref.shape[0]
    subs = c0.shape[1]
    rows_of = c0.shape[2]
    each = slots // subs
    pick = one_hot(target, peers * LANES)
    pieces = (c0, c1, c2, c3)
    for s in range(subs):
        pick_s = pick[:, s * each : (s + 1) * each]
        for i in range(PART):
            stacked = jnp.concatenate([c[i, s] for c in pieces], axis=0)
            moved = lax.dot_general(stacked, pick_s, NT, preferred_element_type=F32).astype(BF16)
            for j in range(BLK):
                for lane in range(LANES):
                    m = lane * PART + i
                    moved_ref[
                        lax.rem(here + j, BLK),
                        s * rows_of : (s + 1) * rows_of,
                        m * peers : (m + 1) * peers,
                    ] = moved[j * rows_of : (j + 1) * rows_of, lane * peers : (lane + 1) * peers]
    total = jnp.zeros((peers, diag.shape[2]), F32)
    for lane in range(LANES):
        total += jnp.dot(
            pick[lane * peers : (lane + 1) * peers], diag[lane], preferred_element_type=F32
        )
    diag_ref[...] = total


def pack_kernel(a0, a1, a2, a3, diag_ref, pay_ref, total, spread):
    peers = diag_ref.shape[0]
    total[...] = (
        (a0[...].astype(F32) + a1[...].astype(F32)) + (a2[...].astype(F32) + a3[...].astype(F32))
    )
    for m in range(MEMBERS):
        spread[pl.ds(m, peers, stride=PAY), :] = total[pl.ds(m, peers, stride=MEMBERS), :]
    spread[pl.ds(MEMBERS, peers, stride=PAY), :] = diag_ref[...]
    spread[pl.ds(MEMBERS + 1, peers, stride=PAY), :] = jnp.zeros_like(diag_ref)
    pay_ref[...] = spread[...].astype(BF16)


def interior_kernel(pay, got, coupling, out, own32, got32, coefs):
    peers = pay.shape[0] // PAY
    own32[...] = pay[...].astype(F32)
    got32[...] = got[...].astype(F32)
    own_diag = own32[pl.ds(MEMBERS, peers, stride=PAY), :]
    both = own_diag + got32[pl.ds(MEMBERS, peers, stride=PAY), :]
    divisor = jnp.where(own_diag > 0.0, both, 1.0)
    for m in range(MEMBERS):
        rows = pl.ds(m, peers, stride=PAY)
        summed = own32[rows, :] + got32[rows, :]
        used = jnp.broadcast_to(own_diag[:, m : m + 1], summed.shape) > 0.0
        below = jnp.broadcast_to(divisor[:, m : m + 1], summed.shape)
        coefs[m * peers : (m + 1) * peers, :] = jnp.where(used, summed / below, 0.0).astype(BF16)
    rows = coupling.shape[0] * coupling.shape[1]
    out[...] = jnp.dot(
        coupling[...].reshape(rows, coupling.shape[2]), coefs[...], preferred_element_type=F32
    ).reshape(out.shape)


def shift(x, by):
    return lax.ppermute(x, "blk", [(i, (i + by) % BLK) for i in range(BLK)])


def local(factor, samples, diagonal, coupling, blocks, peer_device, peer_lane, owns_face):
    peers = lax.axis_size("sub")
    here = lax.axis_index("blk")
    subs, order, quarter = factor.shape
    slot_count = diagonal.shape[1]
    columns = samples.shape[2]
    inner = coupling.shape[1]
    slots = subs * slot_count
    positions = peers * LANES
    vmem = pl.BlockSpec(memory_space=VMEM)
    smem = pl.BlockSpec(memory_space=pltpu.SMEM)

    d2 = shift(samples, 2)
    d3 = shift(samples, 1)
    d1 = shift(samples, -1)

    meta = jnp.concatenate([here[None].astype(jnp.int32), blocks * TILE])
    live = jnp.arange(slot_count, dtype=jnp.int32)[None, :] < blocks[:, None]
    target = jnp.where(live, peer_lane * peers + peer_device, -1).reshape(1, slots)

    grouped = coupling.reshape(subs, inner, slot_count, BLK, PART).transpose(3, 4, 0, 1, 2)
    def turned(j):
        return lax.dynamic_index_in_dim(grouped, lax.rem(here + j, BLK), 0, keepdims=False)
    c0 = turned(0)
    c3 = shift(turned(1), 1)
    c2 = shift(turned(2), 2)
    c1 = shift(turned(3), -1)

    mine = lax.dynamic_slice_in_dim(diagonal.reshape(slots, TILE), here * PART, PART, 1)
    diag = jnp.stack(
        [jnp.pad(mine, ((0, 0), (l * PART, 128 - (l + 1) * PART))) for l in range(LANES)]
    )

    rows = peers * MEMBERS
    piece = jax.ShapeDtypeStruct((rows, columns), BF16)
    o0, o1, o2, o3 = pl.pallas_call(
        traces_kernel,
        out_shape=[piece] * BLK,
        in_specs=[smem] + [vmem] * 5 + [pl.BlockSpec(memory_space=pltpu.HBM)],
        out_specs=[vmem] * BLK,
        scratch_shapes=[
            VMEM(factor.shape, BF16),
            VMEM((subs * order, columns), F32),
            VMEM((BLK, positions * PART, columns), F32),
            pltpu.SemaphoreType.DMA((subs * BLK,)),
        ],
        compiler_params=pltpu.CompilerParams(vmem_limit_bytes=40 << 20),
        cost_estimate=pl.CostEstimate(
            flops=4 * subs * order * quarter * columns, bytes_accessed=8 << 20, transcendentals=0
        ),
        name="traces",
    )(meta, target, samples, d1, d2, d3, factor)

    a2 = shift(o2, 2)
    a1 = shift(o1, 1)
    a3 = shift(o3, -1)

    moved, diag_rows = pl.pallas_call(
        coupling_kernel,
        out_shape=[
            jax.ShapeDtypeStruct((BLK, subs * inner, rows), BF16),
            jax.ShapeDtypeStruct((peers, columns), F32),
        ],
        in_specs=[smem] + [vmem] * 6,
        out_specs=[vmem] * 2,
        compiler_params=pltpu.CompilerParams(vmem_limit_bytes=16 << 20),
        cost_estimate=pl.CostEstimate(flops=1 << 27, bytes_accessed=4 << 20, transcendentals=0),
        name="coupling",
    )(meta, target, diag, c0, c1, c2, c3)

    pay = pl.pallas_call(
        pack_kernel,
        out_shape=jax.ShapeDtypeStruct((peers * PAY, columns), BF16),
        in_specs=[vmem] * 5,
        out_specs=vmem,
        scratch_shapes=[VMEM((rows, columns), F32), VMEM((peers * PAY, columns), F32)],
        compiler_params=pltpu.CompilerParams(vmem_limit_bytes=16 << 20),
        name="pack",
    )(o0, a1, a2, a3, diag_rows)

    got = lax.all_to_all(
        pay.reshape(peers, PAY // 2, 2, columns), "sub", split_axis=0, concat_axis=0, tiled=True
    ).reshape(peers * PAY, columns)

    part = pl.pallas_call(
        interior_kernel,
        out_shape=jax.ShapeDtypeStruct((BLK, subs * inner, columns), F32),
        in_specs=[vmem] * 3,
        out_specs=vmem,
        scratch_shapes=[
            VMEM((peers * PAY, columns), F32),
            VMEM((peers * PAY, columns), F32),
            VMEM((rows, columns), BF16),
        ],
        compiler_params=pltpu.CompilerParams(vmem_limit_bytes=16 << 20),
        name="interior",
    )(pay, got, moved)

    parts = lax.all_to_all(part, "blk", split_axis=0, concat_axis=0, tiled=True)
    return parts.sum(axis=0).astype(BF16).reshape(subs, inner, columns)


def solution(mesh):
    placed = (
        P("sub", None, "blk"),
        P("sub", "blk", None),
        P("sub", None, None),
        P("sub", "blk", None),
        P("sub"),
        P("sub", None),
        P("sub", None),
        P("sub", None),
    )
    return jax.shard_map(
        local, mesh=mesh, in_specs=placed, out_specs=P("sub", "blk", None), check_vma=False
    )
```

```python
import jax
import jax.numpy as jnp
from jax import lax
from jax.experimental import pallas as pl
from jax.experimental.pallas import tpu as pltpu
from jax.sharding import PartitionSpec as P


BF16 = jnp.bfloat16
F32 = jnp.float32
LANES = 2
BLK = 4
TILE = 16
PART = TILE // BLK
MEMBERS = LANES * PART
PAY = MEMBERS + 2

VMEM = pltpu.VMEM
TN = (((0,), (0,)), ((), ()))
NT = (((1,), (1,)), ((), ()))


def one_hot(target_ref, positions):
    slots = target_ref.shape[1]
    rows = lax.broadcasted_iota(jnp.int32, (positions, slots), 0)
    hit = rows == jnp.broadcast_to(target_ref[...], (positions, slots))
    return jnp.where(hit, 1.0, 0.0).astype(BF16)


def products(meta, shards, factor, offsets, accs, ready):
    subs = len(accs)
    for s in range(subs):
        for shard, j in shards:
            rows = offsets[j] + lax.broadcasted_iota(jnp.int32, shard.shape[1:], 0)
            part = jnp.where(rows < meta[1 + s], shard[s].astype(F32), 0.0).astype(BF16)
            ready(s, j)
            piece = lax.dot_general(
                part,
                factor[s, pl.ds(offsets[j], shard.shape[1]), :],
                TN,
                preferred_element_type=F32,
            )
            accs[s] = piece if accs[s] is None else accs[s] + piece
    return accs


def row_offsets(here, quarter):
    return [pl.multiple_of(lax.rem(here + j, BLK) * quarter, quarter) for j in range(BLK)]


def first_kernel(meta, target, diag, d0, factor, fac, acc_ref, diag_ref, sems):
    subs, order, quarter = factor.shape
    offsets = row_offsets(meta[0], quarter)
    copies = {}
    for j in range(BLK):
        for s in range(subs):
            rows = pl.ds(offsets[j], quarter)
            copies[s, j] = pltpu.make_async_copy(
                factor.at[s, rows, :], fac.at[s, rows, :], sems.at[s * BLK + j]
            )
            copies[s, j].start()
    peers = diag_ref.shape[0]
    pick = one_hot(target, peers * LANES)
    total = jnp.zeros(diag_ref.shape, F32)
    for lane in range(LANES):
        total += jnp.dot(
            pick[lane * peers : (lane + 1) * peers], diag[lane], preferred_element_type=F32
        )
    diag_ref[...] = total
    accs = products(
        meta, ((d0, 0),), fac, offsets, [None] * subs, lambda s, j: copies[s, j].wait()
    )
    for s in range(subs):
        acc_ref[s] = accs[s]
        for j in range(1, BLK):
            copies[s, j].wait()


def near_kernel(meta, d1, d3, acc_ref, fac, out_ref):
    offsets = row_offsets(meta[0], fac.shape[2])
    accs = products(
        meta,
        ((d1, 1), (d3, 3)),
        fac,
        offsets,
        [acc_ref[s] for s in range(fac.shape[0])],
        lambda s, j: None,
    )
    for s in range(fac.shape[0]):
        out_ref[s] = accs[s]


def traces_kernel(meta, target, d2, acc_ref, fac, c1, c2, c3, o0, o1, o2, o3, wide, placed):
    subs, order, quarter = fac.shape
    slots = target.shape[1]
    positions = placed.shape[1] // PART
    peers = positions // LANES
    here = meta[0]
    offsets = row_offsets(here, quarter)
    accs = products(
        meta, ((d2, 2),), fac, offsets, [acc_ref[s] for s in range(subs)], lambda s, j: None
    )
    for s in range(subs):
        cols = offsets[0] + lax.broadcasted_iota(jnp.int32, accs[s].shape, 1)
        reduced = jnp.where(cols < meta[1 + s], accs[s], 0.0).astype(BF16)
        wide[pl.ds(s * order, order), :] = lax.dot_general(
            fac[s], reduced, NT, preferred_element_type=F32
        )
    pick = one_hot(target, positions)
    for t in range(TILE):
        rows = wide[pl.ds(t, slots, stride=TILE), :].astype(BF16)
        moved = jnp.dot(pick, rows, preferred_element_type=F32)
        for lane in range(LANES):
            placed[t // PART, pl.ds(lane * PART + t % PART, peers, stride=MEMBERS), :] = moved[
                lane * peers : (lane + 1) * peers
            ]
    count = placed.shape[1]
    for j, out in enumerate((o0, o1, o2, o3)):
        out[:count] = placed[lax.rem(here + j, BLK)].astype(BF16)
    for out, piece in ((o1, c1), (o2, c2), (o3, c3)):
        out[count:] = piece[...]


def pack_kernel(meta, target, diag_ref, c0, a0, a2, a1, a3, pay_ref, moved_ref, total, spread):
    here = meta[0]
    slots = target.shape[1]
    peers = diag_ref.shape[0]
    count = total.shape[0]
    total[...] = (a0[...].astype(F32) + a1[:count].astype(F32)) + (
        a2[:count].astype(F32) + a3[:count].astype(F32)
    )
    for m in range(MEMBERS):
        spread[pl.ds(m, peers, stride=PAY), :] = total[pl.ds(m, peers, stride=MEMBERS), :]
    spread[pl.ds(MEMBERS, peers, stride=PAY), :] = diag_ref[...]
    spread[pl.ds(MEMBERS + 1, peers, stride=PAY), :] = jnp.zeros_like(diag_ref)
    pay_ref[...] = spread[...].astype(BF16)

    both = moved_ref.shape[1]
    each = c0.shape[1]
    subs = slots // each
    rows_of = both // subs
    pick = one_hot(target, peers * LANES)
    pieces = (c0[...], a3[count:], a2[count:], a1[count:])
    for s in range(subs):
        pick_s = pick[:, s * each : (s + 1) * each]
        for i in range(PART):
            low = (i * subs + s) * rows_of
            stacked = jnp.concatenate([c[low : low + rows_of] for c in pieces], axis=0)
            moved = lax.dot_general(stacked, pick_s, NT, preferred_element_type=F32).astype(BF16)
            for j in range(BLK):
                for lane in range(LANES):
                    m = lane * PART + i
                    moved_ref[
                        lax.rem(here + j, BLK),
                        s * rows_of : (s + 1) * rows_of,
                        m * peers : (m + 1) * peers,
                    ] = moved[j * rows_of : (j + 1) * rows_of, lane * peers : (lane + 1) * peers]


def interior_kernel(pay, got, coupling, out, own32, got32, coefs):
    peers = pay.shape[0] // PAY
    own32[...] = pay[...].astype(F32)
    got32[...] = got[...].astype(F32)
    own_diag = own32[pl.ds(MEMBERS, peers, stride=PAY), :]
    both = own_diag + got32[pl.ds(MEMBERS, peers, stride=PAY), :]
    divisor = jnp.where(own_diag > 0.0, both, 1.0)
    for m in range(MEMBERS):
        rows = pl.ds(m, peers, stride=PAY)
        summed = own32[rows, :] + got32[rows, :]
        used = jnp.broadcast_to(own_diag[:, m : m + 1], summed.shape) > 0.0
        below = jnp.broadcast_to(divisor[:, m : m + 1], summed.shape)
        coefs[m * peers : (m + 1) * peers, :] = jnp.where(used, summed / below, 0.0).astype(BF16)
    rows = coupling.shape[0] * coupling.shape[1]
    out[...] = jnp.dot(
        coupling[...].reshape(rows, coupling.shape[2]), coefs[...], preferred_element_type=F32
    ).reshape(out.shape)


def shift(x, by):
    return lax.ppermute(x, "blk", [(i, (i + by) % BLK) for i in range(BLK)])


def local(factor, samples, diagonal, coupling, blocks, peer_device, peer_lane, owns_face):
    peers = lax.axis_size("sub")
    here = lax.axis_index("blk")
    subs, order, quarter = factor.shape
    slot_count = diagonal.shape[1]
    columns = samples.shape[2]
    inner = coupling.shape[1]
    slots = subs * slot_count
    positions = peers * LANES
    vmem = pl.BlockSpec(memory_space=VMEM)
    smem = pl.BlockSpec(memory_space=pltpu.SMEM)

    d1 = shift(samples, -1)
    d3 = shift(samples, 1)
    d2 = shift(samples, 2)

    meta = jnp.concatenate([here[None].astype(jnp.int32), blocks * TILE])
    live = jnp.arange(slot_count, dtype=jnp.int32)[None, :] < blocks[:, None]
    target = jnp.where(live, peer_lane * peers + peer_device, -1).reshape(1, slots)

    grouped = coupling.reshape(subs, inner, slot_count, BLK, PART).transpose(3, 4, 0, 1, 2)

    def turned(j):
        piece = lax.dynamic_index_in_dim(grouped, lax.rem(here + j, BLK), 0, keepdims=False)
        return piece.reshape(PART * subs * inner, slot_count)

    mine = lax.dynamic_slice_in_dim(diagonal.reshape(slots, TILE), here * PART, PART, 1)
    diag = jnp.stack(
        [jnp.pad(mine, ((0, 0), (l * PART, 128 - (l + 1) * PART))) for l in range(LANES)]
    )

    rows = peers * MEMBERS
    extra = PART * subs * inner
    fac, acc, diag_rows = pl.pallas_call(
        first_kernel,
        out_shape=[
            jax.ShapeDtypeStruct(factor.shape, BF16),
            jax.ShapeDtypeStruct((subs, columns, quarter), F32),
            jax.ShapeDtypeStruct((peers, columns), F32),
        ],
        in_specs=[smem] + [vmem] * 3 + [pl.BlockSpec(memory_space=pltpu.HBM)],
        out_specs=[vmem] * 3,
        scratch_shapes=[pltpu.SemaphoreType.DMA((subs * BLK,))],
        compiler_params=pltpu.CompilerParams(vmem_limit_bytes=24 << 20),
        cost_estimate=pl.CostEstimate(
            flops=2 * subs * quarter * quarter * columns, bytes_accessed=4 << 20, transcendentals=0
        ),
        name="first",
    )(meta, target, diag, samples, factor)

    acc = pl.pallas_call(
        near_kernel,
        out_shape=jax.ShapeDtypeStruct((subs, columns, quarter), F32),
        in_specs=[smem] + [vmem] * 4,
        out_specs=vmem,
        compiler_params=pltpu.CompilerParams(vmem_limit_bytes=24 << 20),
        cost_estimate=pl.CostEstimate(
            flops=4 * subs * quarter * quarter * columns, bytes_accessed=4 << 20, transcendentals=0
        ),
        name="near",
    )(meta, d1, d3, acc, fac)

    piece = jax.ShapeDtypeStruct((rows + extra, columns), BF16)
    o0, o1, o2, o3 = pl.pallas_call(
        traces_kernel,
        out_shape=[jax.ShapeDtypeStruct((rows, columns), BF16)] + [piece] * 3,
        in_specs=[smem] + [vmem] * 7,
        out_specs=[vmem] * BLK,
        scratch_shapes=[
            VMEM((subs * order, columns), F32),
            VMEM((BLK, positions * PART, columns), F32),
        ],
        compiler_params=pltpu.CompilerParams(vmem_limit_bytes=32 << 20),
        cost_estimate=pl.CostEstimate(
            flops=4 * subs * order * quarter * columns, bytes_accessed=8 << 20, transcendentals=0
        ),
        name="traces",
    )(meta, target, d2, acc, fac, turned(1), turned(2), turned(3))

    a2 = shift(o2, 2)
    a1 = shift(o1, 1)
    a3 = shift(o3, -1)

    pay, moved = pl.pallas_call(
        pack_kernel,
        out_shape=[
            jax.ShapeDtypeStruct((peers * PAY, columns), BF16),
            jax.ShapeDtypeStruct((BLK, subs * inner, rows), BF16),
        ],
        in_specs=[smem] + [vmem] * 7,
        out_specs=[vmem] * 2,
        scratch_shapes=[VMEM((rows, columns), F32), VMEM((peers * PAY, columns), F32)],
        compiler_params=pltpu.CompilerParams(vmem_limit_bytes=16 << 20),
        name="pack",
    )(meta, target, diag_rows, turned(0), o0, a2, a1, a3)

    got = lax.all_to_all(
        pay.reshape(peers, PAY // 2, 2, columns), "sub", split_axis=0, concat_axis=0, tiled=True
    ).reshape(peers * PAY, columns)

    part = pl.pallas_call(
        interior_kernel,
        out_shape=jax.ShapeDtypeStruct((BLK, subs * inner, columns), F32),
        in_specs=[vmem] * 3,
        out_specs=vmem,
        scratch_shapes=[
            VMEM((peers * PAY, columns), F32),
            VMEM((peers * PAY, columns), F32),
            VMEM((rows, columns), BF16),
        ],
        compiler_params=pltpu.CompilerParams(vmem_limit_bytes=16 << 20),
        name="interior",
    )(pay, got, moved)

    parts = lax.all_to_all(part, "blk", split_axis=0, concat_axis=0, tiled=True)
    return parts.sum(axis=0).astype(BF16).reshape(subs, inner, columns)


def solution(mesh):
    placed = (
        P("sub", None, "blk"),
        P("sub", "blk", None),
        P("sub", None, None),
        P("sub", "blk", None),
        P("sub"),
        P("sub", None),
        P("sub", None),
        P("sub", None),
    )
    return jax.shard_map(
        local, mesh=mesh, in_specs=placed, out_specs=P("sub", "blk", None), check_vma=False
    )
```

```python
import jax
import jax.numpy as jnp
from jax import lax
from jax.experimental import pallas as pl
from jax.experimental.pallas import tpu as pltpu
from jax.sharding import PartitionSpec as P


BF16 = jnp.bfloat16
F32 = jnp.float32
LANES = 2
BLK = 4
TILE = 16
PART = TILE // BLK
MEMBERS = LANES * PART
PAY = MEMBERS + 2
FIRST = 48
FACES = 208

VMEM = pltpu.VMEM
TN = (((0,), (0,)), ((), ()))
NT = (((1,), (1,)), ((), ()))


def targets(blocks, device_ref, lane_ref, s, peers):
    shape = (8, device_ref.shape[1])
    place = jnp.broadcast_to(lane_ref[s : s + 1] * peers + device_ref[s : s + 1], shape)
    live = lax.broadcasted_iota(jnp.int32, shape, 1) < blocks[s]
    return jnp.where(live, place, -1)


def one_hot(target, positions):
    shape = (positions, target.shape[1])
    hit = lax.broadcasted_iota(jnp.int32, shape, 0) == jnp.broadcast_to(target[:1], shape)
    return jnp.where(hit, 1.0, 0.0).astype(BF16)


def products(blocks, shards, factor, offsets, accs, ready):
    subs = len(accs)
    for s in range(subs):
        for shard, j in shards:
            rows = offsets[j] + lax.broadcasted_iota(jnp.int32, shard.shape[1:], 0)
            part = jnp.where(rows < blocks[s] * TILE, shard[s].astype(F32), 0.0).astype(BF16)
            ready(s, j)
            piece = lax.dot_general(
                part,
                factor[s, pl.ds(offsets[j], shard.shape[1]), :],
                TN,
                preferred_element_type=F32,
            )
            accs[s] = piece if accs[s] is None else accs[s] + piece
    return accs


def row_offsets(here, quarter):
    return [pl.multiple_of(lax.rem(here + j, BLK) * quarter, quarter) for j in range(BLK)]


def first_kernel(blocks, device_ref, lane_ref, diag, d0, factor, fac, acc_ref, diag_ref, sems):
    subs, order, quarter = factor.shape
    here = lax.axis_index("blk")
    offsets = row_offsets(here, quarter)
    copies = {}
    for j in range(BLK):
        for s in range(subs):
            rows = pl.ds(offsets[j], quarter)
            copies[s, j] = pltpu.make_async_copy(
                factor.at[s, rows, :], fac.at[s, rows, :], sems.at[s * BLK + j]
            )
            copies[s, j].start()
    peers, width = diag_ref.shape
    total = jnp.zeros(diag_ref.shape, F32)
    row = lax.broadcasted_iota(jnp.int32, (TILE, width), 0)
    col = lax.broadcasted_iota(jnp.int32, (TILE, width), 1)
    for s in range(subs):
        pick = one_hot(targets(blocks, device_ref, lane_ref, s, peers), peers * LANES)
        for lane in range(LANES):
            low = lane * PART
            hit = (col >= low) & (col < low + PART) & (row == here * PART + col - low)
            spread = jnp.where(hit, 1.0, 0.0).astype(BF16)
            found = lax.dot_general(
                pick[lane * peers : (lane + 1) * peers], diag[s], NT, preferred_element_type=F32
            )
            total += jnp.dot(found.astype(BF16), spread, preferred_element_type=F32)
    diag_ref[...] = total
    accs = products(
        blocks, ((d0, 0),), fac, offsets, [None] * subs, lambda s, j: copies[s, j].wait()
    )
    for s in range(subs):
        acc_ref[s] = accs[s]
        for j in range(1, BLK):
            copies[s, j].wait()


def near_kernel(blocks, d1, d3, acc_ref, fac, out_ref):
    offsets = row_offsets(lax.axis_index("blk"), fac.shape[2])
    accs = products(
        blocks,
        ((d1, 1), (d3, 3)),
        fac,
        offsets,
        [acc_ref[s] for s in range(fac.shape[0])],
        lambda s, j: None,
    )
    for s in range(fac.shape[0]):
        out_ref[s] = accs[s]


def traces_kernel(blocks, d2, acc_ref, fac, c1, c2, c3, o0, o1, o2, o3, wide):
    subs, order, quarter = fac.shape
    here = lax.axis_index("blk")
    offsets = row_offsets(here, quarter)
    accs = products(
        blocks, ((d2, 2),), fac, offsets, [acc_ref[s] for s in range(subs)], lambda s, j: None
    )
    start = jnp.int32(0)
    for s in range(subs):
        cols = offsets[0] + lax.broadcasted_iota(jnp.int32, accs[s].shape, 1)
        reduced = jnp.where(cols < blocks[s] * TILE, accs[s], 0.0).astype(BF16)
        wide[pl.ds(pl.multiple_of(start * TILE, TILE), order), :] = lax.dot_general(
            fac[s], reduced, NT, preferred_element_type=F32
        )
        start = start + blocks[s]
    for j, out in enumerate((o0, o1, o2, o3)):
        part = lax.rem(here + j, BLK)
        for i in range(PART):
            rows = wide[pl.ds(part * PART + i, FACES, stride=TILE), :]
            out[i * FACES : (i + 1) * FACES] = rows.astype(BF16)
    for out, piece in ((o1, c1), (o2, c2), (o3, c3)):
        out[PART * FACES :] = piece[...]


def pack_kernel(
    blocks, device_ref, lane_ref, diag_ref, c0, a0, a2, a1, a3, pay_ref, moved_ref, spread
):
    here = lax.axis_index("blk")
    peers, columns = diag_ref.shape
    positions = peers * LANES
    subs, each = device_ref.shape
    slots = subs * each
    natural = [targets(blocks, device_ref, lane_ref, s, peers) for s in range(subs)]
    empty = jnp.full((8, slots - each), -1, jnp.int32)
    lanes = lax.broadcasted_iota(jnp.int32, (8, slots), 1)
    start = blocks[0]
    compact = jnp.concatenate([natural[0], empty], axis=1)
    for s in range(1, subs):
        turned = pltpu.roll(jnp.concatenate([natural[s], empty], axis=1), start, 1)
        compact = jnp.where(lanes < start, compact, turned)
        start = start + blocks[s]
    pick = one_hot(compact, positions)
    none = jnp.zeros((slots - FACES, columns), BF16)
    for i in range(PART):
        r = slice(i * FACES, (i + 1) * FACES)
        total = (a0[r].astype(F32) + a1[r].astype(F32)) + (a2[r].astype(F32) + a3[r].astype(F32))
        rows = jnp.concatenate([total.astype(BF16), none], axis=0)
        moved = jnp.dot(pick, rows, preferred_element_type=F32)
        for lane in range(LANES):
            spread[pl.ds(lane * PART + i, peers, stride=PAY), :] = moved[
                lane * peers : (lane + 1) * peers
            ]
    spread[pl.ds(MEMBERS, peers, stride=PAY), :] = diag_ref[...]
    spread[pl.ds(MEMBERS + 1, peers, stride=PAY), :] = jnp.zeros_like(diag_ref)
    pay_ref[...] = spread[...].astype(BF16)

    count = PART * FACES
    rows_of = moved_ref.shape[1] // subs
    pieces = (c0[...], a3[count:], a2[count:], a1[count:])
    for s in range(subs):
        pick_s = one_hot(natural[s], positions)
        for i in range(PART):
            low = (i * subs + s) * rows_of
            stacked = jnp.concatenate([c[low : low + rows_of] for c in pieces], axis=0)
            moved = lax.dot_general(stacked, pick_s, NT, preferred_element_type=F32).astype(BF16)
            for j in range(BLK):
                for lane in range(LANES):
                    m = lane * PART + i
                    moved_ref[
                        lax.rem(here + j, BLK),
                        s * rows_of : (s + 1) * rows_of,
                        m * peers : (m + 1) * peers,
                    ] = moved[j * rows_of : (j + 1) * rows_of, lane * peers : (lane + 1) * peers]


def interior_kernel(pay, got, coupling, out, own32, got32, coefs):
    peers = pay.shape[0] // PAY
    own32[...] = pay[...].astype(F32)
    got32[...] = got[...].astype(F32)
    own_diag = own32[pl.ds(MEMBERS, peers, stride=PAY), :]
    both = own_diag + got32[pl.ds(MEMBERS, peers, stride=PAY), :]
    divisor = jnp.where(own_diag > 0.0, both, 1.0)
    for m in range(MEMBERS):
        rows = pl.ds(m, peers, stride=PAY)
        summed = own32[rows, :] + got32[rows, :]
        used = jnp.broadcast_to(own_diag[:, m : m + 1], summed.shape) > 0.0
        below = jnp.broadcast_to(divisor[:, m : m + 1], summed.shape)
        coefs[m * peers : (m + 1) * peers, :] = jnp.where(used, summed / below, 0.0).astype(BF16)
    rows = coupling.shape[0] * coupling.shape[1]
    out[...] = jnp.dot(
        coupling[...].reshape(rows, coupling.shape[2]), coefs[...], preferred_element_type=F32
    ).reshape(out.shape)


def shift(x, by):
    return lax.ppermute(x, "blk", [(i, (i + by) % BLK) for i in range(BLK)])


def local(factor, samples, diagonal, coupling, blocks, peer_device, peer_lane, owns_face):
    peers = lax.axis_size("sub")
    here = lax.axis_index("blk")
    subs, order, quarter = factor.shape
    slot_count = diagonal.shape[1]
    columns = samples.shape[2]
    inner = coupling.shape[1]
    vmem = pl.BlockSpec(memory_space=VMEM)
    smem = pl.BlockSpec(memory_space=pltpu.SMEM)

    d1 = shift(samples, -1)
    d3 = shift(samples, 1)
    d2 = shift(samples, 2)

    grouped = coupling.reshape(subs, inner, slot_count, BLK, PART).transpose(3, 4, 0, 1, 2)

    def turned(j):
        piece = lax.dynamic_index_in_dim(grouped, lax.rem(here + j, BLK), 0, keepdims=False)
        return piece.reshape(PART * subs * inner, slot_count)

    rows = peers * MEMBERS
    extra = PART * subs * inner
    fac, acc, diag_rows = pl.pallas_call(
        first_kernel,
        out_shape=[
            jax.ShapeDtypeStruct(factor.shape, BF16),
            jax.ShapeDtypeStruct((subs, columns, quarter), F32),
            jax.ShapeDtypeStruct((peers, columns), F32),
        ],
        in_specs=[smem] + [vmem] * 4 + [pl.BlockSpec(memory_space=pltpu.HBM)],
        out_specs=[vmem] * 3,
        scratch_shapes=[pltpu.SemaphoreType.DMA((subs * BLK,))],
        compiler_params=pltpu.CompilerParams(vmem_limit_bytes=FIRST << 20),
        cost_estimate=pl.CostEstimate(
            flops=2 * subs * quarter * quarter * columns, bytes_accessed=4 << 20, transcendentals=0
        ),
        name="first",
    )(blocks, peer_device, peer_lane, diagonal.transpose(0, 2, 1), samples, factor)

    acc = pl.pallas_call(
        near_kernel,
        out_shape=jax.ShapeDtypeStruct((subs, columns, quarter), F32),
        in_specs=[smem] + [vmem] * 4,
        out_specs=vmem,
        compiler_params=pltpu.CompilerParams(vmem_limit_bytes=24 << 20),
        cost_estimate=pl.CostEstimate(
            flops=4 * subs * quarter * quarter * columns, bytes_accessed=4 << 20, transcendentals=0
        ),
        name="near",
    )(blocks, d1, d3, acc, fac)

    count = PART * FACES
    piece = jax.ShapeDtypeStruct((count + extra, columns), BF16)
    o0, o1, o2, o3 = pl.pallas_call(
        traces_kernel,
        out_shape=[jax.ShapeDtypeStruct((count, columns), BF16)] + [piece] * 3,
        in_specs=[smem] + [vmem] * 6,
        out_specs=[vmem] * BLK,
        scratch_shapes=[VMEM((subs * order, columns), F32)],
        compiler_params=pltpu.CompilerParams(vmem_limit_bytes=32 << 20),
        cost_estimate=pl.CostEstimate(
            flops=4 * subs * order * quarter * columns, bytes_accessed=8 << 20, transcendentals=0
        ),
        name="traces",
    )(blocks, d2, acc, fac, turned(1), turned(2), turned(3))

    a2 = shift(o2, 2)
    a1 = shift(o1, 1)
    a3 = shift(o3, -1)

    pay, moved = pl.pallas_call(
        pack_kernel,
        out_shape=[
            jax.ShapeDtypeStruct((peers * PAY, columns), BF16),
            jax.ShapeDtypeStruct((BLK, subs * inner, rows), BF16),
        ],
        in_specs=[smem] + [vmem] * 8,
        out_specs=[vmem] * 2,
        scratch_shapes=[VMEM((peers * PAY, columns), F32)],
        compiler_params=pltpu.CompilerParams(vmem_limit_bytes=16 << 20),
        name="pack",
    )(blocks, peer_device, peer_lane, diag_rows, turned(0), o0, a2, a1, a3)

    got = lax.all_to_all(
        pay.reshape(peers, PAY // 2, 2, columns), "sub", split_axis=0, concat_axis=0, tiled=True
    ).reshape(peers * PAY, columns)

    part = pl.pallas_call(
        interior_kernel,
        out_shape=jax.ShapeDtypeStruct((BLK, subs * inner, columns), F32),
        in_specs=[vmem] * 3,
        out_specs=vmem,
        scratch_shapes=[
            VMEM((peers * PAY, columns), F32),
            VMEM((peers * PAY, columns), F32),
            VMEM((rows, columns), BF16),
        ],
        compiler_params=pltpu.CompilerParams(vmem_limit_bytes=16 << 20),
        name="interior",
    )(pay, got, moved)

    parts = lax.all_to_all(part, "blk", split_axis=0, concat_axis=0, tiled=True)
    return parts.sum(axis=0).astype(BF16).reshape(subs, inner, columns)


def solution(mesh):
    placed = (
        P("sub", None, "blk"),
        P("sub", "blk", None),
        P("sub", None, None),
        P("sub", "blk", None),
        P("sub"),
        P("sub", None),
        P("sub", None),
        P("sub", None),
    )
    return jax.shard_map(
        local, mesh=mesh, in_specs=placed, out_specs=P("sub", "blk", None), check_vma=False
    )
```

```python
import jax
import jax.numpy as jnp
from jax import lax
from jax.experimental import pallas as pl
from jax.experimental.pallas import tpu as pltpu
from jax.sharding import PartitionSpec as P


BF16 = jnp.bfloat16
F32 = jnp.float32
LANES = 2
BLK = 4
TILE = 16
PART = TILE // BLK
MEMBERS = LANES * PART
PAY = MEMBERS + 2
FIRST = 48
FACES = 208

VMEM = pltpu.VMEM
TN = (((0,), (0,)), ((), ()))
NT = (((1,), (1,)), ((), ()))


def targets(blocks, device_ref, lane_ref, s, peers):
    shape = (8, device_ref.shape[1])
    place = jnp.broadcast_to(lane_ref[s : s + 1] * peers + device_ref[s : s + 1], shape)
    live = lax.broadcasted_iota(jnp.int32, shape, 1) < blocks[s]
    return jnp.where(live, place, -1)


def one_hot(target, positions):
    shape = (positions, target.shape[1])
    hit = lax.broadcasted_iota(jnp.int32, shape, 0) == jnp.broadcast_to(target[:1], shape)
    return jnp.where(hit, 1.0, 0.0).astype(BF16)


def products(blocks, shards, factor, offsets, accs, ready):
    subs = len(accs)
    for s in range(subs):
        for shard, j in shards:
            rows = offsets[j] + lax.broadcasted_iota(jnp.int32, shard.shape[1:], 0)
            part = jnp.where(rows < blocks[s] * TILE, shard[s].astype(F32), 0.0).astype(BF16)
            ready(s, j)
            piece = lax.dot_general(
                part,
                factor[s, pl.ds(offsets[j], shard.shape[1]), :],
                TN,
                preferred_element_type=F32,
            )
            accs[s] = piece if accs[s] is None else accs[s] + piece
    return accs


def row_offsets(here, quarter):
    return [pl.multiple_of(lax.rem(here + j, BLK) * quarter, quarter) for j in range(BLK)]


def first_kernel(blocks, device_ref, lane_ref, diag, d0, factor, fac, acc_ref, diag_ref, sems):
    subs, _, quarter = factor.shape
    here = lax.axis_index("blk")
    offsets = row_offsets(here, quarter)
    copies = {}
    for j in range(BLK):
        for s in range(subs):
            rows = pl.ds(offsets[j], quarter)
            copies[s, j] = pltpu.make_async_copy(
                factor.at[s, rows, :], fac.at[s, rows, :], sems.at[s * BLK + j]
            )
            copies[s, j].start()
    peers, width = diag_ref.shape
    total = jnp.zeros(diag_ref.shape, F32)
    row = lax.broadcasted_iota(jnp.int32, (TILE, width), 0)
    col = lax.broadcasted_iota(jnp.int32, (TILE, width), 1)
    for s in range(subs):
        pick = one_hot(targets(blocks, device_ref, lane_ref, s, peers), peers * LANES)
        for lane in range(LANES):
            low = lane * PART
            hit = (col >= low) & (col < low + PART) & (row == here * PART + col - low)
            spread = jnp.where(hit, 1.0, 0.0).astype(BF16)
            found = lax.dot_general(
                pick[lane * peers : (lane + 1) * peers], diag[s], NT, preferred_element_type=F32
            )
            total += jnp.dot(found.astype(BF16), spread, preferred_element_type=F32)
    diag_ref[...] = total
    accs = products(
        blocks, ((d0, 0),), fac, offsets, [None] * subs, lambda s, j: copies[s, j].wait()
    )
    for s in range(subs):
        acc_ref[s] = accs[s]
        for j in range(1, BLK):
            copies[s, j].wait()


def near_kernel(blocks, d2, d3, acc_ref, fac, out_ref):
    offsets = row_offsets(lax.axis_index("blk"), fac.shape[2])
    accs = products(
        blocks,
        ((d2, 2), (d3, 3)),
        fac,
        offsets,
        [acc_ref[s] for s in range(fac.shape[0])],
        lambda s, j: None,
    )
    for s in range(fac.shape[0]):
        out_ref[s] = accs[s]


def traces_kernel(blocks, d1, acc_ref, fac, c1, c2, c3, o0, o1, o2, o3, wide):
    subs, order, quarter = fac.shape
    here = lax.axis_index("blk")
    offsets = row_offsets(here, quarter)
    accs = products(
        blocks, ((d1, 1),), fac, offsets, [acc_ref[s] for s in range(subs)], lambda s, j: None
    )
    start = jnp.int32(0)
    for s in range(subs):
        cols = offsets[0] + lax.broadcasted_iota(jnp.int32, accs[s].shape, 1)
        reduced = jnp.where(cols < blocks[s] * TILE, accs[s], 0.0).astype(BF16)
        wide[pl.ds(pl.multiple_of(start * TILE, TILE), order), :] = lax.dot_general(
            fac[s], reduced, NT, preferred_element_type=F32
        )
        start = start + blocks[s]
    for j, out in enumerate((o0, o1, o2, o3)):
        part = lax.rem(here + j, BLK)
        for i in range(PART):
            rows = wide[pl.ds(part * PART + i, FACES, stride=TILE), :]
            out[i * FACES : (i + 1) * FACES] = rows.astype(BF16)
    for out, piece in ((o1, c1), (o2, c2), (o3, c3)):
        out[PART * FACES :] = piece[...]


def pack_kernel(
    blocks, device_ref, lane_ref, diag_ref, c0, a0, a2, a1, a3, pay_ref, moved_ref, spread
):
    here = lax.axis_index("blk")
    peers, columns = diag_ref.shape
    positions = peers * LANES
    subs, each = device_ref.shape
    slots = subs * each
    natural = [targets(blocks, device_ref, lane_ref, s, peers) for s in range(subs)]
    empty = jnp.full((8, slots - each), -1, jnp.int32)
    lanes = lax.broadcasted_iota(jnp.int32, (8, slots), 1)
    start = blocks[0]
    compact = jnp.concatenate([natural[0], empty], axis=1)
    for s in range(1, subs):
        turned = pltpu.roll(jnp.concatenate([natural[s], empty], axis=1), start, 1)
        compact = jnp.where(lanes < start, compact, turned)
        start = start + blocks[s]
    pick = one_hot(compact, positions)
    none = jnp.zeros((slots - FACES, columns), BF16)
    for i in range(PART):
        r = slice(i * FACES, (i + 1) * FACES)
        total = (a0[r].astype(F32) + a1[r].astype(F32)) + (a2[r].astype(F32) + a3[r].astype(F32))
        rows = jnp.concatenate([total.astype(BF16), none], axis=0)
        moved = jnp.dot(pick, rows, preferred_element_type=F32)
        for lane in range(LANES):
            spread[pl.ds(lane * PART + i, peers, stride=PAY), :] = moved[
                lane * peers : (lane + 1) * peers
            ]
    spread[pl.ds(MEMBERS, peers, stride=PAY), :] = diag_ref[...]
    spread[pl.ds(MEMBERS + 1, peers, stride=PAY), :] = jnp.zeros_like(diag_ref)
    pay_ref[...] = spread[...].astype(BF16)

    count = PART * FACES
    rows_of = moved_ref.shape[1] // subs
    pieces = (c0[...], a3[count:], a2[count:], a1[count:])
    for s in range(subs):
        pick_s = one_hot(natural[s], positions)
        for i in range(PART):
            low = (i * subs + s) * rows_of
            stacked = jnp.concatenate([c[low : low + rows_of] for c in pieces], axis=0)
            moved = lax.dot_general(stacked, pick_s, NT, preferred_element_type=F32).astype(BF16)
            for j in range(BLK):
                for lane in range(LANES):
                    m = lane * PART + i
                    moved_ref[
                        lax.rem(here + j, BLK),
                        s * rows_of : (s + 1) * rows_of,
                        m * peers : (m + 1) * peers,
                    ] = moved[j * rows_of : (j + 1) * rows_of, lane * peers : (lane + 1) * peers]


def interior_kernel(pay, got, coupling, out, own32, got32, coefs):
    peers = pay.shape[0] // PAY
    own32[...] = pay[...].astype(F32)
    got32[...] = got[...].astype(F32)
    own_diag = own32[pl.ds(MEMBERS, peers, stride=PAY), :]
    both = own_diag + got32[pl.ds(MEMBERS, peers, stride=PAY), :]
    divisor = jnp.where(own_diag > 0.0, both, 1.0)
    for m in range(MEMBERS):
        rows = pl.ds(m, peers, stride=PAY)
        summed = own32[rows, :] + got32[rows, :]
        used = jnp.broadcast_to(own_diag[:, m : m + 1], summed.shape) > 0.0
        below = jnp.broadcast_to(divisor[:, m : m + 1], summed.shape)
        coefs[m * peers : (m + 1) * peers, :] = jnp.where(used, summed / below, 0.0).astype(BF16)
    rows = coupling.shape[0] * coupling.shape[1]
    out[...] = jnp.dot(
        coupling[...].reshape(rows, coupling.shape[2]), coefs[...], preferred_element_type=F32
    ).reshape(out.shape).astype(BF16)


def shift(x, by):
    return lax.ppermute(x, "blk", [(i, (i + by) % BLK) for i in range(BLK)])


def body(factor, samples, diagonal, coupling, blocks, peer_device, peer_lane, owns_face):
    peers = lax.axis_size("sub")
    here = lax.axis_index("blk")
    subs, order, quarter = factor.shape
    slot_count = diagonal.shape[1]
    columns = samples.shape[2]
    inner = coupling.shape[1]
    vmem = pl.BlockSpec(memory_space=VMEM)
    smem = pl.BlockSpec(memory_space=pltpu.SMEM)

    d1 = shift(samples, -1)
    d3 = shift(samples, 1)
    d2 = shift(samples, 2)

    grouped = coupling.reshape(subs, inner, slot_count, BLK, PART).transpose(3, 4, 0, 1, 2)

    def turned(j):
        piece = lax.dynamic_index_in_dim(grouped, lax.rem(here + j, BLK), 0, keepdims=False)
        return piece.reshape(PART * subs * inner, slot_count)

    rows = peers * MEMBERS
    extra = PART * subs * inner
    fac, acc, diag_rows = pl.pallas_call(
        first_kernel,
        out_shape=[
            jax.ShapeDtypeStruct(factor.shape, BF16),
            jax.ShapeDtypeStruct((subs, columns, quarter), F32),
            jax.ShapeDtypeStruct((peers, columns), F32),
        ],
        in_specs=[smem] + [vmem] * 4 + [pl.BlockSpec(memory_space=pltpu.HBM)],
        out_specs=[vmem] * 3,
        scratch_shapes=[pltpu.SemaphoreType.DMA((subs * BLK,))],
        compiler_params=pltpu.CompilerParams(vmem_limit_bytes=FIRST << 20),
        cost_estimate=pl.CostEstimate(
            flops=2 * subs * quarter * quarter * columns, bytes_accessed=4 << 20, transcendentals=0
        ),
        name="first",
    )(blocks, peer_device, peer_lane, diagonal.transpose(0, 2, 1), samples, factor)

    acc = pl.pallas_call(
        near_kernel,
        out_shape=jax.ShapeDtypeStruct((subs, columns, quarter), F32),
        in_specs=[smem] + [vmem] * 4,
        out_specs=vmem,
        compiler_params=pltpu.CompilerParams(vmem_limit_bytes=24 << 20),
        cost_estimate=pl.CostEstimate(
            flops=4 * subs * quarter * quarter * columns, bytes_accessed=4 << 20, transcendentals=0
        ),
        name="near",
    )(blocks, d2, d3, acc, fac)

    count = PART * FACES
    piece = jax.ShapeDtypeStruct((count + extra, columns), BF16)
    o0, o1, o2, o3 = pl.pallas_call(
        traces_kernel,
        out_shape=[jax.ShapeDtypeStruct((count, columns), BF16)] + [piece] * 3,
        in_specs=[smem] + [vmem] * 6,
        out_specs=[vmem] * BLK,
        scratch_shapes=[VMEM((subs * order, columns), F32)],
        compiler_params=pltpu.CompilerParams(vmem_limit_bytes=32 << 20),
        cost_estimate=pl.CostEstimate(
            flops=4 * subs * order * quarter * columns, bytes_accessed=8 << 20, transcendentals=0
        ),
        name="traces",
    )(blocks, d1, acc, fac, turned(1), turned(2), turned(3))

    a2 = shift(o2, 2)
    a1 = shift(o1, 1)
    a3 = shift(o3, -1)

    pay, moved = pl.pallas_call(
        pack_kernel,
        out_shape=[
            jax.ShapeDtypeStruct((peers * PAY, columns), BF16),
            jax.ShapeDtypeStruct((BLK, subs * inner, rows), BF16),
        ],
        in_specs=[smem] + [vmem] * 8,
        out_specs=[vmem] * 2,
        scratch_shapes=[VMEM((peers * PAY, columns), F32)],
        compiler_params=pltpu.CompilerParams(vmem_limit_bytes=16 << 20),
        name="pack",
    )(blocks, peer_device, peer_lane, diag_rows, turned(0), o0, a2, a1, a3)

    got = lax.all_to_all(
        pay.reshape(peers, PAY // 2, 2, columns), "sub", split_axis=0, concat_axis=0, tiled=True
    ).reshape(peers * PAY, columns)

    part = pl.pallas_call(
        interior_kernel,
        out_shape=jax.ShapeDtypeStruct((BLK, subs * inner, columns), BF16),
        in_specs=[vmem] * 3,
        out_specs=vmem,
        scratch_shapes=[
            VMEM((peers * PAY, columns), F32),
            VMEM((peers * PAY, columns), F32),
            VMEM((rows, columns), BF16),
        ],
        compiler_params=pltpu.CompilerParams(vmem_limit_bytes=16 << 20),
        name="interior",
    )(pay, got, moved)

    parts = lax.all_to_all(part, "blk", split_axis=0, concat_axis=0, tiled=True)
    return parts.astype(F32).sum(axis=0).astype(BF16).reshape(subs, inner, columns)


def solution(mesh):
    placed = (
        P("sub", None, "blk"),
        P("sub", "blk", None),
        P("sub", None, None),
        P("sub", "blk", None),
        P("sub"),
        P("sub", None),
        P("sub", None),
        P("sub", None),
    )
    return jax.shard_map(
        body, mesh=mesh, in_specs=placed, out_specs=P("sub", "blk", None), check_vma=False
    )
```

```python
import jax
import jax.numpy as jnp
from jax import lax
from jax.experimental import pallas as pl
from jax.experimental.pallas import tpu as pltpu
from jax.sharding import PartitionSpec as P


BF16 = jnp.bfloat16
F32 = jnp.float32
LANES = 2
BLK = 4
TILE = 16
PART = TILE // BLK
MEMBERS = LANES * PART
PAY = MEMBERS + 2
FIRST = 48
FACES = 208

VMEM = pltpu.VMEM
TN = (((0,), (0,)), ((), ()))
NT = (((1,), (1,)), ((), ()))


def targets(blocks, device_ref, lane_ref, s, peers):
    shape = (8, device_ref.shape[1])
    place = jnp.broadcast_to(lane_ref[s : s + 1] * peers + device_ref[s : s + 1], shape)
    live = lax.broadcasted_iota(jnp.int32, shape, 1) < blocks[s]
    return jnp.where(live, place, -1)


def one_hot(target, positions):
    shape = (positions, target.shape[1])
    hit = lax.broadcasted_iota(jnp.int32, shape, 0) == jnp.broadcast_to(target[:1], shape)
    return jnp.where(hit, 1.0, 0.0).astype(BF16)


def products(blocks, shards, factor, offsets, accs, ready):
    subs = len(accs)
    for s in range(subs):
        for shard, j in shards:
            rows = offsets[j] + lax.broadcasted_iota(jnp.int32, shard.shape[1:], 0)
            part = jnp.where(rows < blocks[s] * TILE, shard[s].astype(F32), 0.0).astype(BF16)
            ready(s, j)
            piece = lax.dot_general(
                part,
                factor[s, pl.ds(offsets[j], shard.shape[1]), :],
                TN,
                preferred_element_type=F32,
            )
            accs[s] = piece if accs[s] is None else accs[s] + piece
    return accs


def row_offsets(here, quarter):
    return [pl.multiple_of(jnp.bitwise_xor(here, j) * quarter, quarter) for j in range(BLK)]


def first_kernel(blocks, device_ref, lane_ref, diag, d0, factor, fac, acc_ref, diag_ref, sems):
    subs, _, quarter = factor.shape
    here = lax.axis_index("blk")
    offsets = row_offsets(here, quarter)
    copies = {}
    for j in range(BLK):
        for s in range(subs):
            rows = pl.ds(offsets[j], quarter)
            copies[s, j] = pltpu.make_async_copy(
                factor.at[s, rows, :], fac.at[s, rows, :], sems.at[s * BLK + j]
            )
            copies[s, j].start()
    peers, width = diag_ref.shape
    total = jnp.zeros(diag_ref.shape, F32)
    row = lax.broadcasted_iota(jnp.int32, (TILE, width), 0)
    col = lax.broadcasted_iota(jnp.int32, (TILE, width), 1)
    for s in range(subs):
        pick = one_hot(targets(blocks, device_ref, lane_ref, s, peers), peers * LANES)
        for lane in range(LANES):
            low = lane * PART
            hit = (col >= low) & (col < low + PART) & (row == here * PART + col - low)
            spread = jnp.where(hit, 1.0, 0.0).astype(BF16)
            found = lax.dot_general(
                pick[lane * peers : (lane + 1) * peers], diag[s], NT, preferred_element_type=F32
            )
            total += jnp.dot(found.astype(BF16), spread, preferred_element_type=F32)
    diag_ref[...] = total
    accs = products(
        blocks, ((d0, 0),), fac, offsets, [None] * subs, lambda s, j: copies[s, j].wait()
    )
    for s in range(subs):
        acc_ref[s] = accs[s]
        for j in range(1, BLK):
            copies[s, j].wait()


def near_kernel(blocks, d2, d1, acc_ref, fac, out_ref):
    offsets = row_offsets(lax.axis_index("blk"), fac.shape[2])
    accs = products(
        blocks,
        ((d2, 2), (d1, 1)),
        fac,
        offsets,
        [acc_ref[s] for s in range(fac.shape[0])],
        lambda s, j: None,
    )
    for s in range(fac.shape[0]):
        out_ref[s] = accs[s]


def traces_kernel(blocks, d3, acc_ref, fac, c1, c2, c3, o0, o1, o2, o3, wide):
    subs, order, quarter = fac.shape
    here = lax.axis_index("blk")
    offsets = row_offsets(here, quarter)
    accs = products(
        blocks, ((d3, 3),), fac, offsets, [acc_ref[s] for s in range(subs)], lambda s, j: None
    )
    start = jnp.int32(0)
    for s in range(subs):
        cols = offsets[0] + lax.broadcasted_iota(jnp.int32, accs[s].shape, 1)
        reduced = jnp.where(cols < blocks[s] * TILE, accs[s], 0.0).astype(BF16)
        wide[pl.ds(pl.multiple_of(start * TILE, TILE), order), :] = lax.dot_general(
            fac[s], reduced, NT, preferred_element_type=F32
        )
        start = start + blocks[s]
    for j, out in enumerate((o0, o1, o2, o3)):
        part = jnp.bitwise_xor(here, j)
        for i in range(PART):
            rows = wide[pl.ds(part * PART + i, FACES, stride=TILE), :]
            out[i * FACES : (i + 1) * FACES] = rows.astype(BF16)
    for out, piece in ((o1, c1), (o2, c2), (o3, c3)):
        out[PART * FACES :] = piece[...]


def pack_kernel(
    blocks, device_ref, lane_ref, diag_ref, c0, a0, a2, a1, a3, pay_ref, moved_ref, spread
):
    here = lax.axis_index("blk")
    peers, columns = diag_ref.shape
    positions = peers * LANES
    subs, each = device_ref.shape
    slots = subs * each
    natural = [targets(blocks, device_ref, lane_ref, s, peers) for s in range(subs)]
    empty = jnp.full((8, slots - each), -1, jnp.int32)
    lanes = lax.broadcasted_iota(jnp.int32, (8, slots), 1)
    start = blocks[0]
    compact = jnp.concatenate([natural[0], empty], axis=1)
    for s in range(1, subs):
        turned = pltpu.roll(jnp.concatenate([natural[s], empty], axis=1), start, 1)
        compact = jnp.where(lanes < start, compact, turned)
        start = start + blocks[s]
    pick = one_hot(compact, positions)
    none = jnp.zeros((slots - FACES, columns), BF16)
    for i in range(PART):
        r = slice(i * FACES, (i + 1) * FACES)
        total = (a0[r].astype(F32) + a1[r].astype(F32)) + (a2[r].astype(F32) + a3[r].astype(F32))
        rows = jnp.concatenate([total.astype(BF16), none], axis=0)
        moved = jnp.dot(pick, rows, preferred_element_type=F32)
        for lane in range(LANES):
            spread[pl.ds(lane * PART + i, peers, stride=PAY), :] = moved[
                lane * peers : (lane + 1) * peers
            ]
    spread[pl.ds(MEMBERS, peers, stride=PAY), :] = diag_ref[...]
    spread[pl.ds(MEMBERS + 1, peers, stride=PAY), :] = jnp.zeros_like(diag_ref)
    pay_ref[...] = spread[...].astype(BF16)

    count = PART * FACES
    rows_of = moved_ref.shape[1] // subs
    pieces = (c0[...], a1[count:], a2[count:], a3[count:])
    for s in range(subs):
        pick_s = one_hot(natural[s], positions)
        for i in range(PART):
            low = (i * subs + s) * rows_of
            stacked = jnp.concatenate([c[low : low + rows_of] for c in pieces], axis=0)
            moved = lax.dot_general(stacked, pick_s, NT, preferred_element_type=F32).astype(BF16)
            for j in range(BLK):
                for lane in range(LANES):
                    m = lane * PART + i
                    moved_ref[
                        jnp.bitwise_xor(here, j),
                        s * rows_of : (s + 1) * rows_of,
                        m * peers : (m + 1) * peers,
                    ] = moved[j * rows_of : (j + 1) * rows_of, lane * peers : (lane + 1) * peers]


def interior_kernel(pay, got, coupling, out, own32, got32, coefs):
    peers = pay.shape[0] // PAY
    own32[...] = pay[...].astype(F32)
    got32[...] = got[...].astype(F32)
    own_diag = own32[pl.ds(MEMBERS, peers, stride=PAY), :]
    both = own_diag + got32[pl.ds(MEMBERS, peers, stride=PAY), :]
    divisor = jnp.where(own_diag > 0.0, both, 1.0)
    for m in range(MEMBERS):
        rows = pl.ds(m, peers, stride=PAY)
        summed = own32[rows, :] + got32[rows, :]
        used = jnp.broadcast_to(own_diag[:, m : m + 1], summed.shape) > 0.0
        below = jnp.broadcast_to(divisor[:, m : m + 1], summed.shape)
        coefs[m * peers : (m + 1) * peers, :] = jnp.where(used, summed / below, 0.0).astype(BF16)
    rows = coupling.shape[0] * coupling.shape[1]
    out[...] = jnp.dot(
        coupling[...].reshape(rows, coupling.shape[2]), coefs[...], preferred_element_type=F32
    ).reshape(out.shape).astype(BF16)


def swap(x, j):
    return lax.ppermute(x, "blk", [(i, i ^ j) for i in range(BLK)])


def body(factor, samples, diagonal, coupling, blocks, peer_device, peer_lane, owns_face):
    peers = lax.axis_size("sub")
    here = lax.axis_index("blk")
    subs, order, quarter = factor.shape
    slot_count = diagonal.shape[1]
    columns = samples.shape[2]
    inner = coupling.shape[1]
    vmem = pl.BlockSpec(memory_space=VMEM)
    smem = pl.BlockSpec(memory_space=pltpu.SMEM)

    d1 = swap(samples, 1)
    d3 = swap(samples, 3)
    d2 = swap(samples, 2)

    grouped = coupling.reshape(subs, inner, slot_count, BLK, PART).transpose(3, 4, 0, 1, 2)

    def turned(j):
        piece = lax.dynamic_index_in_dim(grouped, jnp.bitwise_xor(here, j), 0, keepdims=False)
        return piece.reshape(PART * subs * inner, slot_count)

    rows = peers * MEMBERS
    extra = PART * subs * inner
    fac, acc, diag_rows = pl.pallas_call(
        first_kernel,
        out_shape=[
            jax.ShapeDtypeStruct(factor.shape, BF16),
            jax.ShapeDtypeStruct((subs, columns, quarter), F32),
            jax.ShapeDtypeStruct((peers, columns), F32),
        ],
        in_specs=[smem] + [vmem] * 4 + [pl.BlockSpec(memory_space=pltpu.HBM)],
        out_specs=[vmem] * 3,
        scratch_shapes=[pltpu.SemaphoreType.DMA((subs * BLK,))],
        compiler_params=pltpu.CompilerParams(vmem_limit_bytes=FIRST << 20),
        cost_estimate=pl.CostEstimate(
            flops=2 * subs * quarter * quarter * columns, bytes_accessed=4 << 20, transcendentals=0
        ),
        name="first",
    )(blocks, peer_device, peer_lane, diagonal.transpose(0, 2, 1), samples, factor)

    acc = pl.pallas_call(
        near_kernel,
        out_shape=jax.ShapeDtypeStruct((subs, columns, quarter), F32),
        in_specs=[smem] + [vmem] * 4,
        out_specs=vmem,
        compiler_params=pltpu.CompilerParams(vmem_limit_bytes=24 << 20),
        cost_estimate=pl.CostEstimate(
            flops=4 * subs * quarter * quarter * columns, bytes_accessed=4 << 20, transcendentals=0
        ),
        name="near",
    )(blocks, d2, d1, acc, fac)

    count = PART * FACES
    piece = jax.ShapeDtypeStruct((count + extra, columns), BF16)
    o0, o1, o2, o3 = pl.pallas_call(
        traces_kernel,
        out_shape=[jax.ShapeDtypeStruct((count, columns), BF16)] + [piece] * 3,
        in_specs=[smem] + [vmem] * 6,
        out_specs=[vmem] * BLK,
        scratch_shapes=[VMEM((subs * order, columns), F32)],
        compiler_params=pltpu.CompilerParams(vmem_limit_bytes=32 << 20),
        cost_estimate=pl.CostEstimate(
            flops=4 * subs * order * quarter * columns, bytes_accessed=8 << 20, transcendentals=0
        ),
        name="traces",
    )(blocks, d3, acc, fac, turned(1), turned(2), turned(3))

    a2 = swap(o2, 2)
    a1 = swap(o1, 1)
    a3 = swap(o3, 3)

    pay, moved = pl.pallas_call(
        pack_kernel,
        out_shape=[
            jax.ShapeDtypeStruct((peers * PAY, columns), BF16),
            jax.ShapeDtypeStruct((BLK, subs * inner, rows), BF16),
        ],
        in_specs=[smem] + [vmem] * 8,
        out_specs=[vmem] * 2,
        scratch_shapes=[VMEM((peers * PAY, columns), F32)],
        compiler_params=pltpu.CompilerParams(vmem_limit_bytes=16 << 20),
        name="pack",
    )(blocks, peer_device, peer_lane, diag_rows, turned(0), o0, a2, a1, a3)

    got = lax.all_to_all(
        pay.reshape(peers, PAY // 2, 2, columns), "sub", split_axis=0, concat_axis=0, tiled=True
    ).reshape(peers * PAY, columns)

    part = pl.pallas_call(
        interior_kernel,
        out_shape=jax.ShapeDtypeStruct((BLK, subs * inner, columns), BF16),
        in_specs=[vmem] * 3,
        out_specs=vmem,
        scratch_shapes=[
            VMEM((peers * PAY, columns), F32),
            VMEM((peers * PAY, columns), F32),
            VMEM((rows, columns), BF16),
        ],
        compiler_params=pltpu.CompilerParams(vmem_limit_bytes=16 << 20),
        name="interior",
    )(pay, got, moved)

    parts = lax.all_to_all(part, "blk", split_axis=0, concat_axis=0, tiled=True)
    return parts.astype(F32).sum(axis=0).astype(BF16).reshape(subs, inner, columns)


def solution(mesh):
    placed = (
        P("sub", None, "blk"),
        P("sub", "blk", None),
        P("sub", None, None),
        P("sub", "blk", None),
        P("sub"),
        P("sub", None),
        P("sub", None),
        P("sub", None),
    )
    return jax.shard_map(
        body, mesh=mesh, in_specs=placed, out_specs=P("sub", "blk", None), check_vma=False
    )
```

```python
import jax
import jax.numpy as jnp
from jax import lax
from jax.experimental import pallas as pl
from jax.experimental.pallas import tpu as pltpu
from jax.sharding import PartitionSpec as P


BF16 = jnp.bfloat16
F32 = jnp.float32
LANES = 2
BLK = 4
TILE = 16
PART = TILE // BLK
MEMBERS = LANES * PART
PAY = MEMBERS + 2
FIRST = 48
FACES = 208

VMEM = pltpu.VMEM
TN = (((0,), (0,)), ((), ()))
NT = (((1,), (1,)), ((), ()))


def targets(blocks, device_ref, lane_ref, s, peers):
    shape = (8, device_ref.shape[1])
    place = jnp.broadcast_to(lane_ref[s : s + 1] * peers + device_ref[s : s + 1], shape)
    live = lax.broadcasted_iota(jnp.int32, shape, 1) < blocks[s]
    return jnp.where(live, place, -1)


def one_hot(target, positions):
    shape = (positions, target.shape[1])
    hit = lax.broadcasted_iota(jnp.int32, shape, 0) == jnp.broadcast_to(target[:1], shape)
    return jnp.where(hit, 1.0, 0.0).astype(BF16)


def products(blocks, shards, factor, offsets, accs, ready):
    subs = len(accs)
    for s in range(subs):
        for shard, j in shards:
            rows = offsets[j] + lax.broadcasted_iota(jnp.int32, shard.shape[1:], 0)
            part = jnp.where(rows < blocks[s] * TILE, shard[s].astype(F32), 0.0).astype(BF16)
            ready(s, j)
            piece = lax.dot_general(
                part,
                factor[s, pl.ds(offsets[j], shard.shape[1]), :],
                TN,
                preferred_element_type=F32,
            )
            accs[s] = piece if accs[s] is None else accs[s] + piece
    return accs


def row_offsets(here, quarter):
    return [pl.multiple_of(jnp.bitwise_xor(here, j) * quarter, quarter) for j in range(BLK)]


def first_kernel(blocks, device_ref, lane_ref, diag, d0, factor, fac, acc_ref, diag_ref, sems):
    subs, _, quarter = factor.shape
    here = lax.axis_index("blk")
    offsets = row_offsets(here, quarter)
    copies = {}
    for j in range(BLK):
        for s in range(subs):
            rows = pl.ds(offsets[j], quarter)
            copies[s, j] = pltpu.make_async_copy(
                factor.at[s, rows, :], fac.at[s, rows, :], sems.at[s * BLK + j]
            )
            copies[s, j].start()
    peers, width = diag_ref.shape
    total = jnp.zeros(diag_ref.shape, F32)
    row = lax.broadcasted_iota(jnp.int32, (TILE, width), 0)
    col = lax.broadcasted_iota(jnp.int32, (TILE, width), 1)
    for s in range(subs):
        pick = one_hot(targets(blocks, device_ref, lane_ref, s, peers), peers * LANES)
        for lane in range(LANES):
            low = lane * PART
            hit = (col >= low) & (col < low + PART) & (row == here * PART + col - low)
            spread = jnp.where(hit, 1.0, 0.0).astype(BF16)
            found = lax.dot_general(
                pick[lane * peers : (lane + 1) * peers], diag[s], NT, preferred_element_type=F32
            )
            total += jnp.dot(found.astype(BF16), spread, preferred_element_type=F32)
    diag_ref[...] = total
    accs = products(
        blocks, ((d0, 0),), fac, offsets, [None] * subs, lambda s, j: copies[s, j].wait()
    )
    for s in range(subs):
        acc_ref[s] = accs[s]
        for j in range(1, BLK):
            copies[s, j].wait()


def near_kernel(blocks, d2, d3, acc_ref, fac, out_ref):
    offsets = row_offsets(lax.axis_index("blk"), fac.shape[2])
    accs = products(
        blocks,
        ((d2, 2), (d3, 3)),
        fac,
        offsets,
        [acc_ref[s] for s in range(fac.shape[0])],
        lambda s, j: None,
    )
    for s in range(fac.shape[0]):
        out_ref[s] = accs[s]


def traces_kernel(blocks, d1, acc_ref, fac, c1, c2, c3, o0, o1, o2, o3, wide):
    subs, order, quarter = fac.shape
    here = lax.axis_index("blk")
    offsets = row_offsets(here, quarter)
    accs = products(
        blocks, ((d1, 1),), fac, offsets, [acc_ref[s] for s in range(subs)], lambda s, j: None
    )
    start = jnp.int32(0)
    for s in range(subs):
        cols = offsets[0] + lax.broadcasted_iota(jnp.int32, accs[s].shape, 1)
        reduced = jnp.where(cols < blocks[s] * TILE, accs[s], 0.0).astype(BF16)
        wide[pl.ds(pl.multiple_of(start * TILE, TILE), order), :] = lax.dot_general(
            fac[s], reduced, NT, preferred_element_type=F32
        )
        start = start + blocks[s]
    for j, out in enumerate((o0, o1, o2, o3)):
        part = jnp.bitwise_xor(here, j)
        for i in range(PART):
            rows = wide[pl.ds(part * PART + i, FACES, stride=TILE), :]
            out[i * FACES : (i + 1) * FACES] = rows.astype(BF16)
    for out, piece in ((o1, c1), (o2, c2), (o3, c3)):
        out[PART * FACES :] = piece[...]


def pack_kernel(
    blocks, device_ref, lane_ref, diag_ref, c0, a0, a2, a1, a3, pay_ref, moved_ref, spread
):
    here = lax.axis_index("blk")
    peers, columns = diag_ref.shape
    positions = peers * LANES
    subs, each = device_ref.shape
    slots = subs * each
    natural = [targets(blocks, device_ref, lane_ref, s, peers) for s in range(subs)]
    empty = jnp.full((8, slots - each), -1, jnp.int32)
    lanes = lax.broadcasted_iota(jnp.int32, (8, slots), 1)
    start = blocks[0]
    compact = jnp.concatenate([natural[0], empty], axis=1)
    for s in range(1, subs):
        turned = pltpu.roll(jnp.concatenate([natural[s], empty], axis=1), start, 1)
        compact = jnp.where(lanes < start, compact, turned)
        start = start + blocks[s]
    pick = one_hot(compact, positions)
    none = jnp.zeros((slots - FACES, columns), BF16)
    for i in range(PART):
        r = slice(i * FACES, (i + 1) * FACES)
        total = (a0[r].astype(F32) + a1[r].astype(F32)) + (a2[r].astype(F32) + a3[r].astype(F32))
        rows = jnp.concatenate([total.astype(BF16), none], axis=0)
        moved = jnp.dot(pick, rows, preferred_element_type=F32)
        for lane in range(LANES):
            spread[pl.ds(lane * PART + i, peers, stride=PAY), :] = moved[
                lane * peers : (lane + 1) * peers
            ]
    spread[pl.ds(MEMBERS, peers, stride=PAY), :] = diag_ref[...]
    spread[pl.ds(MEMBERS + 1, peers, stride=PAY), :] = jnp.zeros_like(diag_ref)
    pay_ref[...] = spread[...].astype(BF16)

    count = PART * FACES
    rows_of = moved_ref.shape[1] // subs
    pieces = (c0[...], a1[count:], a2[count:], a3[count:])
    for s in range(subs):
        pick_s = one_hot(natural[s], positions)
        for i in range(PART):
            low = (i * subs + s) * rows_of
            stacked = jnp.concatenate([c[low : low + rows_of] for c in pieces], axis=0)
            moved = lax.dot_general(stacked, pick_s, NT, preferred_element_type=F32).astype(BF16)
            for j in range(BLK):
                for lane in range(LANES):
                    m = lane * PART + i
                    moved_ref[
                        jnp.bitwise_xor(here, j),
                        s * rows_of : (s + 1) * rows_of,
                        m * peers : (m + 1) * peers,
                    ] = moved[j * rows_of : (j + 1) * rows_of, lane * peers : (lane + 1) * peers]


def interior_kernel(pay, got, coupling, out, own32, got32, coefs):
    peers = pay.shape[0] // PAY
    own32[...] = pay[...].astype(F32)
    got32[...] = got[...].astype(F32)
    own_diag = own32[pl.ds(MEMBERS, peers, stride=PAY), :]
    both = own_diag + got32[pl.ds(MEMBERS, peers, stride=PAY), :]
    divisor = jnp.where(own_diag > 0.0, both, 1.0)
    for m in range(MEMBERS):
        rows = pl.ds(m, peers, stride=PAY)
        summed = own32[rows, :] + got32[rows, :]
        used = jnp.broadcast_to(own_diag[:, m : m + 1], summed.shape) > 0.0
        below = jnp.broadcast_to(divisor[:, m : m + 1], summed.shape)
        coefs[m * peers : (m + 1) * peers, :] = jnp.where(used, summed / below, 0.0).astype(BF16)
    rows = coupling.shape[0] * coupling.shape[1]
    out[...] = jnp.dot(
        coupling[...].reshape(rows, coupling.shape[2]), coefs[...], preferred_element_type=F32
    ).reshape(out.shape).astype(BF16)


def swap(x, j):
    return lax.ppermute(x, "blk", [(i, i ^ j) for i in range(BLK)])


def body(factor, samples, diagonal, coupling, blocks, peer_device, peer_lane, owns_face):
    peers = lax.axis_size("sub")
    here = lax.axis_index("blk")
    subs, order, quarter = factor.shape
    slot_count = diagonal.shape[1]
    columns = samples.shape[2]
    inner = coupling.shape[1]
    vmem = pl.BlockSpec(memory_space=VMEM)
    smem = pl.BlockSpec(memory_space=pltpu.SMEM)

    d1 = swap(samples, 1)
    d3 = swap(samples, 3)
    d2 = swap(samples, 2)

    grouped = coupling.reshape(subs, inner, slot_count, BLK, PART).transpose(3, 4, 0, 1, 2)

    def turned(j):
        piece = lax.dynamic_index_in_dim(grouped, jnp.bitwise_xor(here, j), 0, keepdims=False)
        return piece.reshape(PART * subs * inner, slot_count)

    rows = peers * MEMBERS
    extra = PART * subs * inner
    fac, acc, diag_rows = pl.pallas_call(
        first_kernel,
        out_shape=[
            jax.ShapeDtypeStruct(factor.shape, BF16),
            jax.ShapeDtypeStruct((subs, columns, quarter), F32),
            jax.ShapeDtypeStruct((peers, columns), F32),
        ],
        in_specs=[smem] + [vmem] * 4 + [pl.BlockSpec(memory_space=pltpu.HBM)],
        out_specs=[vmem] * 3,
        scratch_shapes=[pltpu.SemaphoreType.DMA((subs * BLK,))],
        compiler_params=pltpu.CompilerParams(vmem_limit_bytes=FIRST << 20),
        cost_estimate=pl.CostEstimate(
            flops=2 * subs * quarter * quarter * columns, bytes_accessed=4 << 20, transcendentals=0
        ),
        name="first",
    )(blocks, peer_device, peer_lane, diagonal.transpose(0, 2, 1), samples, factor)

    acc = pl.pallas_call(
        near_kernel,
        out_shape=jax.ShapeDtypeStruct((subs, columns, quarter), F32),
        in_specs=[smem] + [vmem] * 4,
        out_specs=vmem,
        compiler_params=pltpu.CompilerParams(vmem_limit_bytes=24 << 20),
        cost_estimate=pl.CostEstimate(
            flops=4 * subs * quarter * quarter * columns, bytes_accessed=4 << 20, transcendentals=0
        ),
        name="near",
    )(blocks, d2, d3, acc, fac)

    count = PART * FACES
    piece = jax.ShapeDtypeStruct((count + extra, columns), BF16)
    o0, o1, o2, o3 = pl.pallas_call(
        traces_kernel,
        out_shape=[jax.ShapeDtypeStruct((count, columns), BF16)] + [piece] * 3,
        in_specs=[smem] + [vmem] * 6,
        out_specs=[vmem] * BLK,
        scratch_shapes=[VMEM((subs * order, columns), F32)],
        compiler_params=pltpu.CompilerParams(vmem_limit_bytes=32 << 20),
        cost_estimate=pl.CostEstimate(
            flops=4 * subs * order * quarter * columns, bytes_accessed=8 << 20, transcendentals=0
        ),
        name="traces",
    )(blocks, d1, acc, fac, turned(1), turned(2), turned(3))

    a2 = swap(o2, 2)
    a1 = swap(o1, 1)
    a3 = swap(o3, 3)

    pay, moved = pl.pallas_call(
        pack_kernel,
        out_shape=[
            jax.ShapeDtypeStruct((peers * PAY, columns), BF16),
            jax.ShapeDtypeStruct((BLK, subs * inner, rows), BF16),
        ],
        in_specs=[smem] + [vmem] * 8,
        out_specs=[vmem] * 2,
        scratch_shapes=[VMEM((peers * PAY, columns), F32)],
        compiler_params=pltpu.CompilerParams(vmem_limit_bytes=16 << 20),
        name="pack",
    )(blocks, peer_device, peer_lane, diag_rows, turned(0), o0, a2, a1, a3)

    got = lax.all_to_all(
        pay.reshape(peers, PAY // 2, 2, columns), "sub", split_axis=0, concat_axis=0, tiled=True
    ).reshape(peers * PAY, columns)

    part = pl.pallas_call(
        interior_kernel,
        out_shape=jax.ShapeDtypeStruct((BLK, subs * inner, columns), BF16),
        in_specs=[vmem] * 3,
        out_specs=vmem,
        scratch_shapes=[
            VMEM((peers * PAY, columns), F32),
            VMEM((peers * PAY, columns), F32),
            VMEM((rows, columns), BF16),
        ],
        compiler_params=pltpu.CompilerParams(vmem_limit_bytes=16 << 20),
        name="interior",
    )(pay, got, moved)

    parts = lax.all_to_all(part, "blk", split_axis=0, concat_axis=0, tiled=True)
    return parts.astype(F32).sum(axis=0).astype(BF16).reshape(subs, inner, columns)


def solution(mesh):
    placed = (
        P("sub", None, "blk"),
        P("sub", "blk", None),
        P("sub", None, None),
        P("sub", "blk", None),
        P("sub"),
        P("sub", None),
        P("sub", None),
        P("sub", None),
    )
    return jax.shard_map(
        body, mesh=mesh, in_specs=placed, out_specs=P("sub", "blk", None), check_vma=False
    )
```
